32 devices in a mesh: group: 2 (over x), tile: 4 (over y, core), orient: 4 (over z).
Axes of the slice: x: 2, y: 2, z: 4, core: 2. Of those that a mesh axis runs over, the one named last changes fastest.
Arguments:
- micrograph: float32 [768, 1024], P('group', 'tile'), parts along dimension 0, may hold values from -30 to 30
- templates: float32 [4, 4, 128, 128], P('orient', 'tile'), may hold values from 0 to 0.0107421875
- orient_ids: int32 [4, 4], P('orient', 'tile'), may hold values from 0 to 15, as said below
- log_weight: float32 [16], replicated, may hold values from -2 to 2
- ice_mask: int32 [32, 64], P('group', 'tile'), parts along dimension 0, may hold values 0 or 1
Outputs:
- score_map: float32 [512, 1024], P(('group', 'orient'), 'tile'), parts along dimension 0
The draws below stay inside these ranges and needn't reach their ends.
There are 2 independent parts, one for each index of `group`. The reference program is written for one: setup_inputs(seed, part) draws one part's arguments, and reference() takes and returns one part's arrays. A program takes and returns all parts, laid end to end along the dimension named above; an argument that names none is the same for every part. Nothing has to cross between parts.
Inputs may be any that keep to these rules, and one draw needn't show every extreme that they name: `orient_ids`: every slot holds a different orientation.
All inputs are finite; a program needn't handle non-finite values. No bound on the sum of `ice_mask` on one device may be relied on, other than what follows from the above.
Results may differ from the reference program's by a relative error of at most 0.00024.
Values sent between devices are 32-bit elements; how exact they have to be, the bound alone decides.
A program may use at most 64 MiB of HBM per device.

```python
import jax
import jax.numpy as jnp
from jax import lax

TILE = 256
GUARD = 64
TPL = 128
MBLK = 16
EXT = 384
ORI_CYCLE = 4
ORI_BLOCKS = 4
ORIENTS = 16
WIDTH = 1024
N_TILE = 4


def bright_patches(third_key, fourth_key):
    row_starts = jax.random.randint(third_key, (3,), 0, min(TILE, EXT - TPL + 1))
    col_starts = jax.random.randint(fourth_key, (3,), 0, WIDTH - TPL + 1)
    row_grid = jnp.arange(EXT, dtype=jnp.int32)[:, None]
    col_grid = jnp.arange(WIDTH, dtype=jnp.int32)[None, :]
    strengths = jnp.array([120.0, 200.0, 300.0], jnp.float32) / (0.75 * TPL)
    bright = jnp.zeros((EXT, WIDTH), jnp.float32)
    for which in range(3):
        inside = (row_grid >= row_starts[which]) & (row_grid < row_starts[which] + TPL)
        inside = inside & (col_grid >= col_starts[which]) & (col_grid < col_starts[which] + TPL)
        bright = bright + jnp.where(inside, strengths[which], 0.0)
    return bright


def draw_micrograph(key, part):
    first_key, second_key, third_key, fourth_key = jax.random.split(key, 4)
    columns = jnp.arange(WIDTH, dtype=jnp.float32)
    ramp = 1.0 + 2.0 * columns[None, :] / max(WIDTH - 1, 1)
    rough = jax.random.uniform(second_key, (EXT, WIDTH), jnp.float32, 0.6, 1.6)
    bright = bright_patches(third_key, fourth_key)
    base = jnp.clip(jax.random.normal(first_key, (EXT, WIDTH), jnp.float32), -4.0, 4.0)
    field = base * ramp * rough + bright
    return jnp.clip(field, -30.0, 30.0)


def draw_templates(key, part):
    first_key, second_key = jax.random.split(key)
    scales = jax.random.uniform(first_key, (ORI_BLOCKS, ORI_CYCLE, 1, 1), jnp.float32, 0.9, 1.1)
    values = jax.random.uniform(second_key, (ORI_BLOCKS, ORI_CYCLE, TPL, TPL), jnp.float32, 0.0, 1.0)
    return scales * (0.25 + values) / TPL


def draw_orient_ids(key, part):
    order = jax.random.permutation(key, jnp.arange(ORIENTS, dtype=jnp.int32))
    return order.reshape(ORI_BLOCKS, ORI_CYCLE).astype(jnp.int32)


def set_ends(result, rng, least, top_value):
    place = [jax.random.randint(jax.random.fold_in(rng, axis), (), 0, length) for axis, length in enumerate(result.shape)]
    widest = result.shape.index(max(result.shape))
    neighbour = place[:widest] + [(place[widest] + 1) % result.shape[widest]] + place[widest + 1:]
    return result.at[tuple(place)].set(least).at[tuple(neighbour)].set(top_value)


def setup_inputs(seed: int = 0, part: int = 0) -> dict:
    seeds = jax.random.split(jax.random.key(seed), 6)
    part_keys = jax.random.split(jax.random.fold_in(seeds[5], part), 6)
    micrograph = draw_micrograph(jax.random.fold_in(jax.random.fold_in(seeds[5], part), 71), part)
    templates = draw_templates(jax.random.fold_in(seeds[5], 71), part)
    orient_ids = draw_orient_ids(jax.random.fold_in(seeds[5], 71), part)
    log_weight = jnp.clip(jax.random.uniform(seeds[3], (ORIENTS,), jnp.float32, -2.0, 2.0), -2.0, 2.0)
    ice_mask = set_ends((jax.random.randint(part_keys[4], (TILE // MBLK, WIDTH // MBLK), 0, 4) < 1).astype(jnp.int32), jax.random.fold_in(part_keys[4], 1), 0, 1)
    return dict(micrograph=micrograph, templates=templates, orient_ids=orient_ids, log_weight=log_weight, ice_mask=ice_mask)


def reference(micrograph, templates, orient_ids, log_weight, ice_mask):
    padded = jnp.pad(micrograph, ((0, 0), (GUARD, GUARD)))
    flat_templates = templates.reshape(ORIENTS, TPL, TPL)
    template_spec = jnp.fft.rfft2(flat_templates, s=(EXT, EXT))
    weights = log_weight[orient_ids.reshape(-1)]

    def one_tile(tile_index):
        window = lax.dynamic_slice_in_dim(padded, tile_index * TILE, EXT, 1)
        window_spec = jnp.fft.rfft2(window)
        correlation = jnp.fft.irfft2(window_spec[None] * jnp.conj(template_spec), s=(EXT, EXT))[:, :TILE, :TILE]
        scores = correlation + weights[:, None, None]
        return jax.scipy.special.logsumexp(scores, axis=0)
    per_tile = lax.map(one_tile, jnp.arange(N_TILE, dtype=jnp.int32))
    log_total = jnp.transpose(per_tile, (1, 0, 2)).reshape(TILE, WIDTH)
    blocks = jnp.repeat(jnp.repeat(ice_mask, MBLK, axis=0), MBLK, axis=1)
    unmasked = 1.0 - blocks.astype(jnp.float32)
    live_count = jnp.sum(unmasked)
    average = jnp.sum(unmasked * log_total) / live_count
    variance = jnp.sum(unmasked * (log_total - average) ** 2) / live_count
    return unmasked * (log_total - average) / jnp.sqrt(variance + 1e-05)
```

```python
import functools
import math

import jax
import jax.numpy as jnp
import numpy as np
from jax import lax
from jax.experimental import pallas as pl
from jax.experimental.pallas import tpu as pltpu
from jax.sharding import PartitionSpec as P

MBLK = 16
F32 = jnp.float32
BF16 = jnp.bfloat16
MESH = pl.DeviceIdType.MESH


def halves(table):
    table = jnp.asarray(table, F32) if isinstance(table, jax.Array) else table.astype(np.float32)
    high = table.astype(jnp.bfloat16)
    low = (table - high.astype(np.float32)).astype(jnp.bfloat16)
    return np.concatenate([high, low], axis=0)


def tables(patch):
    length = 2 * patch
    n = np.arange(length)[:, None]
    k = np.arange(patch)[None, :]
    theta = 2 * math.pi * ((n * (2 * k + 1)) % (2 * length)) / (2 * length)
    tx = np.concatenate([np.cos(theta), -np.sin(theta)], axis=1)
    back = theta[:patch].T
    ix = np.concatenate([np.cos(back), -np.sin(back)], axis=0) * (2.0 / length)
    m = np.arange(length)
    phi = 2 * math.pi * ((m[:, None] * m[None, :]) % length) / length
    c, s = np.cos(phi), np.sin(phi)
    ty = np.block([[c, s], [-s, c]])
    cp, sp = c[:, :patch], s[:, :patch]
    tt = np.block([[cp, sp], [-sp, cp]])
    ci, si = c[:patch], s[:patch]
    iy = np.block([[ci, -si], [si, ci]]) / length
    return tuple(halves(t) for t in (tx, ix, ty, tt, iy))


def split(value):
    high = value.astype(BF16)
    low = (value - high.astype(F32)).astype(BF16)
    return high, low


def dot(a, b):
    return jnp.dot(a, b, preferred_element_type=F32)


def left_table(table, high, low):
    rows = table.shape[0] // 2
    both = dot(table[...], high)
    return both[:rows] + both[rows:] + dot(table[:rows, :], low)


def right_table(value, table):
    rows = value.shape[0]
    depth = table.shape[0] // 2
    high, low = split(value)
    both = dot(jnp.concatenate([high, low], axis=0), table[:depth, :])
    return both[:rows] + both[rows:] + dot(high, table[depth:, :])


def kernel(
    tiles, orients, guard,
    mic, tpl, ids, logw, mask, tx, ix, ty, tt, iy,
    out,
    halo_l, halo_r, stack, wbuf, img, spec, scores, lse_out, lse_in, stats,
    halo_send, halo_recv, tpl_send, tpl_recv, w_send, w_recv,
    lse_send, lse_recv, st_send, st_recv,
):
    t = lax.axis_index("tile")
    o = lax.axis_index("orient")
    everyone = tiles * orients
    me = t * orients + o
    extent, side = mic.shape
    patch = tpl.shape[2]
    length = 2 * patch
    blocks = side // patch
    share = out.shape[0]

    barrier = pltpu.get_barrier_semaphore()

    def greet(k, carry):
        peer = lax.rem(me + k, everyone)
        pl.semaphore_signal(
            barrier, inc=1,
            device_id={"tile": peer // orients, "orient": lax.rem(peer, orients)},
            device_id_type=MESH,
        )
        return carry

    lax.fori_loop(1, everyone, greet, 0)

    wbuf[0] = jnp.full(wbuf.shape[1:], logw[ids[0, 0]], F32)
    stack[0] = tpl[0, 0]

    pl.semaphore_wait(barrier, everyone - 1)

    def halo_copy(src, dst, side_index, peer):
        return pltpu.make_async_remote_copy(
            src_ref=src, dst_ref=dst, send_sem=halo_send.at[side_index],
            recv_sem=halo_recv.at[side_index], device_id={"tile": peer}, device_id_type=MESH,
        )

    to_right = halo_copy(mic.at[:, side - patch:], halo_l, 0, lax.rem(t + 1, tiles))
    to_left = halo_copy(mic.at[:, :patch], halo_r, 1, lax.rem(t + tiles - 1, tiles))

    @pl.when(t < tiles - 1)
    def _():
        to_right.start()

    @pl.when(t > 0)
    def _():
        to_left.start()

    def tpl_copy(k):
        return pltpu.make_async_remote_copy(
            src_ref=tpl.at[0, 0], dst_ref=stack.at[k], send_sem=tpl_send.at[k],
            recv_sem=tpl_recv.at[k], device_id={"tile": lax.rem(t + k, tiles)},
            device_id_type=MESH,
        )

    def w_copy(k):
        return pltpu.make_async_remote_copy(
            src_ref=wbuf.at[0], dst_ref=wbuf.at[k], send_sem=w_send.at[k],
            recv_sem=w_recv.at[k], device_id={"tile": lax.rem(t + k, tiles)},
            device_id_type=MESH,
        )

    for k in range(1, tiles):
        tpl_copy(k).start()
    for k in range(1, tiles):
        w_copy(k).start()

    mask_rows, mask_cols = mask.shape
    row_id = lax.broadcasted_iota(jnp.int32, (share, mask_rows), 0) + o * share
    pick = lax.broadcasted_iota(jnp.int32, (share, mask_rows), 1)
    low_edge = pick * MBLK
    rows_of = jnp.where((row_id >= low_edge) & (row_id < low_edge + MBLK), 1.0, 0.0).astype(F32)
    col_id = lax.broadcasted_iota(jnp.int32, (mask_cols, side), 1)
    col_edge = lax.broadcasted_iota(jnp.int32, (mask_cols, side), 0) * MBLK
    cols_of = jnp.where((col_id >= col_edge) & (col_id < col_edge + MBLK), 1.0, 0.0).astype(F32)
    unmasked = 1.0 - dot(dot(rows_of, mask[...].astype(F32)), cols_of)

    @pl.when(t < tiles - 1)
    def _():
        to_right.wait_send()
        to_left.wait_recv()

    @pl.when(t == tiles - 1)
    def _():
        halo_r[...] = jnp.zeros(halo_r.shape, F32)

    @pl.when(t > 0)
    def _():
        to_left.wait_send()
        to_right.wait_recv()

    @pl.when(t == 0)
    def _():
        halo_l[...] = jnp.zeros(halo_l.shape, F32)

    rolled = [halo_l[...]] + [mic[:, b * patch:(b + 1) * patch] for b in range(blocks)] + [halo_r[...]]
    rolled = [pltpu.roll(part, guard, 1) for part in rolled]
    lane = lax.broadcasted_iota(jnp.int32, (extent, patch), 1)
    ext = [jnp.where(lane < guard, rolled[b], rolled[b + 1]) for b in range(blocks + 1)]
    real, imag = [], []
    for b in range(blocks):
        half = right_table(jnp.concatenate([ext[b], ext[b + 1]], axis=1), tx)
        real.append(half[:, :patch])
        imag.append(half[:, patch:])
    real_high, real_low = split(jnp.concatenate(real, axis=1))
    imag_high, imag_low = split(jnp.concatenate(imag, axis=1))
    for a in range(blocks):
        rows = slice(a * patch, a * patch + length)
        img[a] = left_table(
            ty,
            jnp.concatenate([real_high[rows], imag_high[rows]], axis=0),
            jnp.concatenate([real_low[rows], imag_low[rows]], axis=0),
        )

    tx_head = jnp.concatenate([tx[:patch, :], tx[length:length + patch, :]], axis=0)

    def one_template(k):
        half = right_table(stack[k], tx_head)
        high, low = split(jnp.concatenate([half[:, :patch], half[:, patch:]], axis=0))
        sp = left_table(tt, high, low)
        sr, si = sp[:length], sp[length:]
        wide_r = jnp.concatenate([sr] * blocks, axis=1)
        wide_i = jnp.concatenate([si] * blocks, axis=1)
        weight = wbuf[k][:1, :1]
        for a in range(blocks):
            ir, ii = img[a, :length, :], img[a, length:, :]
            cross = jnp.concatenate([ir * wide_r + ii * wide_i, ii * wide_r - ir * wide_i], axis=0)
            high, low = split(cross)
            mid = left_table(iy, high, low)
            pieces = jnp.concatenate(
                [
                    jnp.concatenate(
                        [mid[:patch, b * patch:(b + 1) * patch], mid[patch:, b * patch:(b + 1) * patch]],
                        axis=1,
                    )
                    for b in range(blocks)
                ],
                axis=0,
            )
            final = right_table(pieces, ix) + weight
            for b in range(blocks):
                scores[k, a * patch:(a + 1) * patch, b * patch:(b + 1) * patch] = final[
                    b * patch:(b + 1) * patch
                ]

    if tiles <= 4:
        for k in range(tiles):
            if k:
                tpl_copy(k).wait()
                w_copy(k).wait()
            one_template(k)
    else:
        for k in range(1, tiles):
            tpl_copy(k).wait()
            w_copy(k).wait()

        def step(k, carry):
            one_template(k)
            return carry

        lax.fori_loop(0, tiles, step, 0)

    def own_lse(owner):
        rows = pl.ds(pl.multiple_of(owner * share, share), share)
        top = scores[0, rows, :]
        for k in range(1, tiles):
            top = jnp.maximum(top, scores[k, rows, :])
        total = jnp.exp(scores[0, rows, :] - top)
        for k in range(1, tiles):
            total = total + jnp.exp(scores[k, rows, :] - top)
        return top + jnp.log(total)

    def lse_copy(k):
        return pltpu.make_async_remote_copy(
            src_ref=lse_out.at[k], dst_ref=lse_in.at[k], send_sem=lse_send.at[k],
            recv_sem=lse_recv.at[k], device_id={"orient": lax.rem(o + k, orients)},
            device_id_type=MESH,
        )

    for k in range(1, orients):
        lse_out[k] = own_lse(lax.rem(o + k, orients))
        lse_copy(k).start()
    mine = own_lse(o)
    for k in range(1, orients):
        lse_copy(k).wait()
    top = mine
    for k in range(1, orients):
        top = jnp.maximum(top, lse_in[k])
    total = jnp.exp(mine - top)
    for k in range(1, orients):
        total = total + jnp.exp(lse_in[k] - top)
    lse = top + jnp.log(total)

    def whole_sum(value):
        return jnp.sum(jnp.sum(value, axis=0, keepdims=True), axis=1, keepdims=True)

    count = whole_sum(unmasked)
    sum_here = whole_sum(unmasked * lse)
    mean_here = sum_here / jnp.maximum(count, 1.0)
    deviation = lse - mean_here
    squares = whole_sum(unmasked * deviation * deviation)
    lane = lax.broadcasted_iota(jnp.int32, stats.shape[1:], 1)
    stats[0] = jnp.where(
        lane == 0, count, jnp.where(lane == 1, sum_here, jnp.where(lane == 2, squares, 0.0))
    )

    def st_copy(k):
        peer = lax.rem(me + k, everyone)
        return pltpu.make_async_remote_copy(
            src_ref=stats.at[0], dst_ref=stats.at[k], send_sem=st_send.at[k],
            recv_sem=st_recv.at[k],
            device_id={"tile": peer // orients, "orient": lax.rem(peer, orients)},
            device_id_type=MESH,
        )

    def st_start(k, carry):
        st_copy(k).start()
        return carry

    def st_wait(k, carry):
        st_copy(k).wait()
        return carry

    lax.fori_loop(1, everyone, st_start, 0)
    lax.fori_loop(1, everyone, st_wait, 0)
    table = stats[:, 0, :]
    counts, sums, sqs = table[:, 0:1], table[:, 1:2], table[:, 2:3]
    live = jnp.sum(counts, axis=0, keepdims=True)
    average = jnp.sum(sums, axis=0, keepdims=True) / live
    gap = sums / jnp.maximum(counts, 1.0) - average
    variance = jnp.sum(sqs + counts * gap * gap, axis=0, keepdims=True) / live
    out[...] = unmasked * (lse - average) / jnp.sqrt(variance + 1e-05)


def body(tiles, orients, micrograph, templates, orient_ids, log_weight, ice_mask):
    extent, side = micrograph.shape
    patch = templates.shape[2]
    share = side // orients
    blocks = side // patch
    everyone = tiles * orients
    vmem = pl.BlockSpec(memory_space=pltpu.VMEM)
    smem = pl.BlockSpec(memory_space=pltpu.SMEM)
    dma = pltpu.SemaphoreType.DMA
    consts = [jnp.asarray(table) for table in tables(patch)]
    return pl.pallas_call(
        functools.partial(kernel, tiles, orients, patch // 2),
        out_shape=jax.ShapeDtypeStruct((share, side), F32),
        in_specs=[vmem, vmem, smem, smem, vmem] + [vmem] * len(consts),
        out_specs=vmem,
        scratch_shapes=[
            pltpu.VMEM((extent, patch), F32),
            pltpu.VMEM((extent, patch), F32),
            pltpu.VMEM((tiles, patch, patch), F32),
            pltpu.VMEM((tiles, 8, 128), F32),
            pltpu.VMEM((blocks, 4 * patch, side), F32),
            pltpu.VMEM((8, 128), F32),
            pltpu.VMEM((tiles, side, side), F32),
            pltpu.VMEM((orients, share, side), F32),
            pltpu.VMEM((orients, share, side), F32),
            pltpu.VMEM((everyone, 8, 128), F32),
            dma((2,)), dma((2,)),
            dma((tiles,)), dma((tiles,)), dma((tiles,)), dma((tiles,)),
            dma((orients,)), dma((orients,)),
            dma((everyone,)), dma((everyone,)),
        ],
        compiler_params=pltpu.CompilerParams(
            collective_id=0, has_side_effects=True, vmem_limit_bytes=56 * 1024 * 1024
        ),
    )(micrograph, templates, orient_ids, log_weight, ice_mask, *consts)


def solution(mesh):
    return jax.shard_map(
        functools.partial(body, mesh.shape["tile"], mesh.shape["orient"]),
        mesh=mesh,
        in_specs=(
            P("group", "tile"),
            P("orient", "tile", None, None),
            P("orient", "tile"),
            P(),
            P("group", "tile"),
        ),
        out_specs=P(("group", "orient"), "tile"),
        check_vma=False,
    )
```

```python
import functools
import math

import jax
import jax.numpy as jnp
import numpy as np
from jax import lax
from jax.experimental import pallas as pl
from jax.experimental.pallas import tpu as pltpu
from jax.sharding import PartitionSpec as P

MBLK = 16
F32 = jnp.float32
BF16 = jnp.bfloat16
MESH = pl.DeviceIdType.MESH


def halves(table):
    table = jnp.asarray(table, F32) if isinstance(table, jax.Array) else table.astype(np.float32)
    high = table.astype(jnp.bfloat16)
    low = (table - high.astype(np.float32)).astype(jnp.bfloat16)
    return np.concatenate([high, low], axis=0)


def tables(patch):
    length = 2 * patch
    n = np.arange(length)[:, None]
    k = np.arange(patch)[None, :]
    theta = 2 * math.pi * ((n * (2 * k + 1)) % (2 * length)) / (2 * length)
    tx = np.concatenate([np.cos(theta), -np.sin(theta)], axis=1)
    back = theta[:patch].T
    ix = np.concatenate([np.cos(back), -np.sin(back)], axis=0) * (2.0 / length)
    m = np.arange(length)
    phi = 2 * math.pi * ((m[:, None] * m[None, :]) % length) / length
    c, s = np.cos(phi), np.sin(phi)
    ty = np.block([[c, s], [-s, c]])
    cp, sp = c[:, :patch], s[:, :patch]
    tt = np.block([[cp, sp], [-sp, cp]])
    ci, si = c[:patch], s[:patch]
    iy = np.block([[ci, -si], [si, ci]]) / length
    return tuple(halves(t) for t in (tx, ix, ty, tt, iy))


def split(value):
    high = value.astype(BF16)
    low = (value - high.astype(F32)).astype(BF16)
    return high, low


def dot(a, b):
    return jnp.dot(a, b, preferred_element_type=F32)


def left_table(table, high, low):
    rows = table.shape[0] // 2
    both = dot(table[...], high)
    return both[:rows] + both[rows:] + dot(table[:rows, :], low)


def right_table(value, table):
    rows = value.shape[0]
    depth = table.shape[0] // 2
    high, low = split(value)
    both = dot(jnp.concatenate([high, low], axis=0), table[:depth, :])
    return both[:rows] + both[rows:] + dot(high, table[depth:, :])


def kernel(
    tiles, orients, guard,
    mic, tpl, ids, logw, mask, tx_any, ix_any, ty_any, tt_any, iy_any,
    out,
    tx, ix, ty, tt, iy, pack_l, pack_r,
    halo_l, halo_r, stack, wbuf, img, spec, scores, lse_out, lse_in, stats,
    table_sem,
    halo_send, halo_recv, tpl_send, tpl_recv, w_send, w_recv,
    lse_send, lse_recv, st_send, st_recv,
):
    t = lax.axis_index("tile")
    o = lax.axis_index("orient")
    everyone = tiles * orients
    me = t * orients + o
    extent, side = mic.shape
    patch = tpl.shape[2]
    length = 2 * patch
    blocks = side // patch
    share = out.shape[0]

    barrier = pltpu.get_barrier_semaphore()

    def greet(k, carry):
        peer = lax.rem(me + k, everyone)
        pl.semaphore_signal(
            barrier, inc=1,
            device_id={"tile": peer // orients, "orient": lax.rem(peer, orients)},
            device_id_type=MESH,
        )
        return carry

    lax.fori_loop(1, everyone, greet, 0)

    loads = {}
    order = (("tx", tx_any, tx), ("tt", tt_any, tt), ("ty", ty_any, ty), ("ix", ix_any, ix), ("iy", iy_any, iy))
    for index, (name, source, target) in enumerate(order):
        loads[name] = pltpu.make_async_copy(source, target, table_sem.at[index])
        loads[name].start()

    known = lax.broadcasted_iota(jnp.int32, (1, logw.shape[1]), 1) == ids[...]
    weight = jnp.sum(jnp.where(known, logw[...], 0.0), axis=1, keepdims=True)
    wbuf[0] = jnp.broadcast_to(weight, wbuf.shape[1:])
    stack[0] = tpl[0, 0]

    middle = extent // 2
    lane_half = lax.broadcasted_iota(jnp.int32, (middle, patch), 1) < guard
    outer, inner = mic[:, side - patch:], mic[:, :patch]
    pack_r[...] = jnp.where(lane_half, pltpu.roll(outer[:middle], guard, 1), outer[middle:])
    pack_l[...] = jnp.where(lane_half, inner[:middle], pltpu.roll(inner[middle:], guard, 1))

    loads["tx"].wait()
    loads["tt"].wait()
    tx_head = jnp.concatenate([tx[:patch, :], tx[length:length + patch, :]], axis=0)

    def spectrum(k):
        half = right_table(stack[k], tx_head)
        high, low = split(jnp.concatenate([half[:, :patch], half[:, patch:]], axis=0))
        spec[k] = left_table(tt, high, low)

    spectrum(0)

    pl.semaphore_wait(barrier, everyone - 1)

    def halo_copy(src, dst, side_index, peer):
        return pltpu.make_async_remote_copy(
            src_ref=src, dst_ref=dst, send_sem=halo_send.at[side_index],
            recv_sem=halo_recv.at[side_index], device_id={"tile": peer}, device_id_type=MESH,
        )

    to_right = halo_copy(pack_r, halo_l, 0, lax.rem(t + 1, tiles))
    to_left = halo_copy(pack_l, halo_r, 1, lax.rem(t + tiles - 1, tiles))

    @pl.when(t < tiles - 1)
    def _():
        to_right.start()

    @pl.when(t > 0)
    def _():
        to_left.start()

    def partner(k):
        if tiles & (tiles - 1):
            return lax.rem(t + k, tiles)
        bit, peer = 1, 0
        while bit < tiles:
            peer = peer + lax.rem(t // bit + k // bit, 2) * bit
            bit *= 2
        return peer

    def tpl_copy(k):
        return pltpu.make_async_remote_copy(
            src_ref=tpl.at[0, 0], dst_ref=stack.at[k], send_sem=tpl_send.at[k],
            recv_sem=tpl_recv.at[k], device_id={"tile": partner(k)},
            device_id_type=MESH,
        )

    def w_copy(k):
        return pltpu.make_async_remote_copy(
            src_ref=wbuf.at[0], dst_ref=wbuf.at[k], send_sem=w_send.at[k],
            recv_sem=w_recv.at[k], device_id={"tile": partner(k)},
            device_id_type=MESH,
        )

    tpl_copy(1).start()
    for k in range(1, tiles):
        w_copy(k).start()

    mask_rows, mask_cols = mask.shape
    row_id = lax.broadcasted_iota(jnp.int32, (share, mask_rows), 0) + o * share
    pick = lax.broadcasted_iota(jnp.int32, (share, mask_rows), 1)
    low_edge = pick * MBLK
    rows_of = jnp.where((row_id >= low_edge) & (row_id < low_edge + MBLK), 1.0, 0.0).astype(F32)
    col_id = lax.broadcasted_iota(jnp.int32, (mask_cols, side), 1)
    col_edge = lax.broadcasted_iota(jnp.int32, (mask_cols, side), 0) * MBLK
    cols_of = jnp.where((col_id >= col_edge) & (col_id < col_edge + MBLK), 1.0, 0.0).astype(F32)
    unmasked = 1.0 - dot(dot(rows_of, mask[...].astype(F32)), cols_of)

    tpl_copy(1).wait()
    spectrum(1)

    @pl.when(t < tiles - 1)
    def _():
        to_right.wait_send()
        to_left.wait_recv()

    @pl.when(t == tiles - 1)
    def _():
        halo_r[...] = jnp.zeros(halo_r.shape, F32)

    @pl.when(t > 0)
    def _():
        to_left.wait_send()
        to_right.wait_recv()

    @pl.when(t == 0)
    def _():
        halo_l[...] = jnp.zeros(halo_l.shape, F32)

    for k in range(2, tiles):
        tpl_copy(k).start()

    left, right = halo_l[...], halo_r[...]
    rolled = [pltpu.roll(mic[:, b * patch:(b + 1) * patch], guard, 1) for b in range(blocks)]
    rolled = (
        [jnp.concatenate([left, pltpu.roll(left, guard, 1)], axis=0)]
        + rolled
        + [jnp.concatenate([pltpu.roll(right, guard, 1), right], axis=0)]
    )
    lane = lax.broadcasted_iota(jnp.int32, (extent, patch), 1)
    ext = [jnp.where(lane < guard, rolled[b], rolled[b + 1]) for b in range(blocks + 1)]
    real, imag = [], []
    for b in range(blocks):
        half = right_table(jnp.concatenate([ext[b], ext[b + 1]], axis=1), tx)
        real.append(half[:, :patch])
        imag.append(half[:, patch:])
    real_high, real_low = split(jnp.concatenate(real, axis=1))
    imag_high, imag_low = split(jnp.concatenate(imag, axis=1))
    loads["ty"].wait()
    for a in range(blocks):
        rows = slice(a * patch, a * patch + length)
        img[a] = left_table(
            ty,
            jnp.concatenate([real_high[rows], imag_high[rows]], axis=0),
            jnp.concatenate([real_low[rows], imag_low[rows]], axis=0),
        )

    loads["ix"].wait()
    loads["iy"].wait()

    def correlate(k, a):
        sr, si = spec[k, :length], spec[k, length:]
        wide_r = jnp.concatenate([sr] * blocks, axis=1)
        wide_i = jnp.concatenate([si] * blocks, axis=1)
        weight = wbuf[k][:1, :1]
        ir, ii = img[a, :length, :], img[a, length:, :]
        cross = jnp.concatenate([ir * wide_r + ii * wide_i, ii * wide_r - ir * wide_i], axis=0)
        high, low = split(cross)
        mid = left_table(iy, high, low)
        pieces = jnp.concatenate(
            [
                jnp.concatenate(
                    [mid[:patch, b * patch:(b + 1) * patch], mid[patch:, b * patch:(b + 1) * patch]],
                    axis=1,
                )
                for b in range(blocks)
            ],
            axis=0,
        )
        final = right_table(pieces, ix) + weight
        for b in range(blocks):
            scores[k, :, b * patch:(b + 1) * patch] = final[b * patch:(b + 1) * patch]

    def own_lse(place):
        rows = pl.ds(pl.multiple_of(place * share, share), share)
        top = scores[0, rows, :]
        for k in range(1, tiles):
            top = jnp.maximum(top, scores[k, rows, :])
        total = jnp.exp(scores[0, rows, :] - top)
        for k in range(1, tiles):
            total = total + jnp.exp(scores[k, rows, :] - top)
        return top + jnp.log(total)

    def lse_copy(k):
        return pltpu.make_async_remote_copy(
            src_ref=lse_out.at[k], dst_ref=lse_in.at[k], send_sem=lse_send.at[k],
            recv_sem=lse_recv.at[k], device_id={"orient": lax.rem(o + k, orients)},
            device_id_type=MESH,
        )

    owners = patch // share
    home, seat = o // owners, lax.rem(o, owners)

    def send_rows(a, place):
        ahead = lax.rem(a * owners + place - o + orients, orients)
        lse_out[ahead] = own_lse(place)
        lse_copy(ahead).start()

    for s in range(blocks):
        a = lax.rem(home + 1 + s, blocks)
        if tiles <= 4:
            for k in range(tiles):
                if s == 0 and k:
                    w_copy(k).wait()
                if s == 0 and k > 1:
                    tpl_copy(k).wait()
                    spectrum(k)
                correlate(k, a)
        else:
            if s == 0:
                w_copy(1).wait()
                for k in range(2, tiles):
                    tpl_copy(k).wait()
                    w_copy(k).wait()

                def later(k, carry):
                    spectrum(k)
                    return carry

                lax.fori_loop(2, tiles, later, 0)

            def step(k, carry):
                correlate(k, a)
                return carry

            lax.fori_loop(0, tiles, step, 0)
        if s < blocks - 1:
            for place in range(owners):
                send_rows(a, place)
        else:
            for gap in range(1, owners):
                send_rows(a, lax.rem(seat + gap, owners))
    mine = own_lse(seat)
    for k in range(1, orients):
        lse_copy(k).wait()
    top = mine
    for k in range(1, orients):
        top = jnp.maximum(top, lse_in[k])
    total = jnp.exp(mine - top)
    for k in range(1, orients):
        total = total + jnp.exp(lse_in[k] - top)
    lse = top + jnp.log(total)

    def whole_sum(value):
        return jnp.sum(jnp.sum(value, axis=0, keepdims=True), axis=1, keepdims=True)

    count = whole_sum(unmasked)
    sum_here = whole_sum(unmasked * lse)
    mean_here = sum_here / jnp.maximum(count, 1.0)
    deviation = lse - mean_here
    squares = whole_sum(unmasked * deviation * deviation)
    lane = lax.broadcasted_iota(jnp.int32, stats.shape[1:], 1)
    stats[0] = jnp.where(
        lane == 0, count, jnp.where(lane == 1, sum_here, jnp.where(lane == 2, squares, 0.0))
    )

    def st_copy(k):
        peer = lax.rem(me + k, everyone)
        return pltpu.make_async_remote_copy(
            src_ref=stats.at[0], dst_ref=stats.at[k], send_sem=st_send.at[k],
            recv_sem=st_recv.at[k],
            device_id={"tile": peer // orients, "orient": lax.rem(peer, orients)},
            device_id_type=MESH,
        )

    def st_start(k, carry):
        st_copy(k).start()
        return carry

    def st_wait(k, carry):
        st_copy(k).wait()
        return carry

    lax.fori_loop(1, everyone, st_start, 0)
    lax.fori_loop(1, everyone, st_wait, 0)
    table = stats[:, 0, :]
    counts, sums, sqs = table[:, 0:1], table[:, 1:2], table[:, 2:3]
    live = jnp.sum(counts, axis=0, keepdims=True)
    average = jnp.sum(sums, axis=0, keepdims=True) / live
    gap = sums / jnp.maximum(counts, 1.0) - average
    variance = jnp.sum(sqs + counts * gap * gap, axis=0, keepdims=True) / live
    out[...] = unmasked * (lse - average) / jnp.sqrt(variance + 1e-05)


def body(tiles, orients, micrograph, templates, orient_ids, log_weight, ice_mask):
    extent, side = micrograph.shape
    patch = templates.shape[2]
    share = side // orients
    blocks = side // patch
    everyone = tiles * orients
    vmem = pl.BlockSpec(memory_space=pltpu.VMEM)
    dma = pltpu.SemaphoreType.DMA
    consts = [jnp.asarray(table) for table in tables(patch)]
    return pl.pallas_call(
        functools.partial(kernel, tiles, orients, patch // 2),
        out_shape=jax.ShapeDtypeStruct((share, side), F32),
        in_specs=[vmem] * 5 + [pl.BlockSpec(memory_space=pl.ANY)] * len(consts),
        out_specs=vmem,
        scratch_shapes=[
            *[pltpu.VMEM(table.shape, BF16) for table in consts],
            pltpu.VMEM((extent // 2, patch), F32),
            pltpu.VMEM((extent // 2, patch), F32),
            pltpu.VMEM((extent // 2, patch), F32),
            pltpu.VMEM((extent // 2, patch), F32),
            pltpu.VMEM((tiles, patch, patch), F32),
            pltpu.VMEM((tiles, 8, 128), F32),
            pltpu.VMEM((blocks, 4 * patch, side), F32),
            pltpu.VMEM((tiles, 4 * patch, patch), F32),
            pltpu.VMEM((tiles, patch, side), F32),
            pltpu.VMEM((orients, share, side), F32),
            pltpu.VMEM((orients, share, side), F32),
            pltpu.VMEM((everyone, 8, 128), F32),
            dma((len(consts),)),
            dma((2,)), dma((2,)),
            dma((tiles,)), dma((tiles,)), dma((tiles,)), dma((tiles,)),
            dma((orients,)), dma((orients,)),
            dma((everyone,)), dma((everyone,)),
        ],
        compiler_params=pltpu.CompilerParams(
            collective_id=0, has_side_effects=True, vmem_limit_bytes=56 * 1024 * 1024
        ),
    )(micrograph, templates, orient_ids, log_weight.reshape(1, -1), ice_mask, *consts)


def solution(mesh):
    return jax.shard_map(
        functools.partial(body, mesh.shape["tile"], mesh.shape["orient"]),
        mesh=mesh,
        in_specs=(
            P("group", "tile"),
            P("orient", "tile", None, None),
            P("orient", "tile"),
            P(),
            P("group", "tile"),
        ),
        out_specs=P(("group", "orient"), "tile"),
        check_vma=False,
    )
```

```python
import functools
import math

import jax
import jax.numpy as jnp
import numpy as np
from jax import lax
from jax.experimental import pallas as pl
from jax.experimental.pallas import tpu as pltpu
from jax.sharding import PartitionSpec as P

MBLK = 16
F32 = jnp.float32
BF16 = jnp.bfloat16
MESH = pl.DeviceIdType.MESH


def halves(table):
    table = jnp.asarray(table, F32) if isinstance(table, jax.Array) else table.astype(np.float32)
    high = table.astype(jnp.bfloat16)
    low = (table - high.astype(np.float32)).astype(jnp.bfloat16)
    return np.concatenate([high, low], axis=0)


def tables(patch):
    length = 2 * patch
    n = np.arange(length)[:, None]
    k = np.arange(patch)[None, :]
    theta = 2 * math.pi * ((n * (2 * k + 1)) % (2 * length)) / (2 * length)
    tx = np.concatenate([np.cos(theta), -np.sin(theta)], axis=1)
    back = theta[:patch].T
    ix = np.concatenate([np.cos(back), -np.sin(back)], axis=0) * (2.0 / length)
    m = np.arange(length)
    phi = 2 * math.pi * ((m[:, None] * m[None, :]) % length) / length
    c, s = np.cos(phi), np.sin(phi)
    ty = np.block([[c, s], [-s, c]])
    cp, sp = c[:, :patch], s[:, :patch]
    tt = np.block([[cp, sp], [-sp, cp]])
    ci, si = c[:patch], s[:patch]
    iy = np.block([[ci, -si], [si, ci]]) / length
    return tuple(halves(t) for t in (tx, ix, ty, tt, iy))


def split(value):
    high = value.astype(BF16)
    low = (value - high.astype(F32)).astype(BF16)
    return high, low


def dot(a, b):
    return jnp.dot(a, b, preferred_element_type=F32)


def left_table(table, high, low):
    rows = table.shape[0] // 2
    both = dot(table[...], high)
    return both[:rows] + both[rows:] + dot(table[:rows, :], low)


def right_table(value, table):
    rows = value.shape[0]
    depth = table.shape[0] // 2
    high, low = split(value)
    both = dot(jnp.concatenate([high, low], axis=0), table[:depth, :])
    return both[:rows] + both[rows:] + dot(high, table[depth:, :])


def kernel(
    tiles, orients, guard,
    mic, tpl, ids, logw, mask, tx_any, ix_any, ty_any, tt_any, iy_any,
    out,
    tx, ix, ty, tt, iy, pack_l, pack_r,
    halo_l, halo_r, stack, wbuf, img, spec, scores, lse_out, lse_in, stats,
    table_sem,
    halo_send, halo_recv, tpl_send, tpl_recv, w_send, w_recv,
    lse_send, lse_recv, st_send, st_recv,
):
    t = lax.axis_index("tile")
    o = lax.axis_index("orient")
    everyone = tiles * orients
    me = t * orients + o
    extent, side = mic.shape
    patch = tpl.shape[2]
    length = 2 * patch
    blocks = side // patch
    share = out.shape[0]

    barrier = pltpu.get_barrier_semaphore()

    def greet(k, carry):
        peer = lax.rem(me + k, everyone)
        pl.semaphore_signal(
            barrier, inc=1,
            device_id={"tile": peer // orients, "orient": lax.rem(peer, orients)},
            device_id_type=MESH,
        )
        return carry

    lax.fori_loop(1, everyone, greet, 0)

    loads = {}
    order = (("tx", tx_any, tx), ("tt", tt_any, tt), ("ty", ty_any, ty), ("ix", ix_any, ix), ("iy", iy_any, iy))
    for index, (name, source, target) in enumerate(order):
        loads[name] = pltpu.make_async_copy(source, target, table_sem.at[index])
        loads[name].start()

    known = lax.broadcasted_iota(jnp.int32, (1, logw.shape[1]), 1) == ids[...]
    weight = jnp.sum(jnp.where(known, logw[...], 0.0), axis=1, keepdims=True)
    wbuf[0] = jnp.broadcast_to(weight, wbuf.shape[1:])
    stack[0] = tpl[0, 0]

    middle = extent // 2
    lane_half = lax.broadcasted_iota(jnp.int32, (middle, patch), 1) < guard
    outer, inner = mic[:, side - patch:], mic[:, :patch]
    pack_r[...] = jnp.where(lane_half, pltpu.roll(outer[:middle], guard, 1), outer[middle:])
    pack_l[...] = jnp.where(lane_half, inner[:middle], pltpu.roll(inner[middle:], guard, 1))

    loads["tx"].wait()
    loads["tt"].wait()
    tx_head = jnp.concatenate([tx[:patch, :], tx[length:length + patch, :]], axis=0)

    def spectrum(k):
        half = right_table(stack[k], tx_head)
        high, low = split(jnp.concatenate([half[:, :patch], half[:, patch:]], axis=0))
        spec[k] = left_table(tt, high, low)

    spectrum(0)

    pl.semaphore_wait(barrier, everyone - 1)

    def halo_copy(src, dst, side_index, peer):
        return pltpu.make_async_remote_copy(
            src_ref=src, dst_ref=dst, send_sem=halo_send.at[side_index],
            recv_sem=halo_recv.at[side_index], device_id={"tile": peer}, device_id_type=MESH,
        )

    to_right = halo_copy(pack_r, halo_l, 0, lax.rem(t + 1, tiles))
    to_left = halo_copy(pack_l, halo_r, 1, lax.rem(t + tiles - 1, tiles))

    @pl.when(t < tiles - 1)
    def _():
        to_right.start()

    @pl.when(t > 0)
    def _():
        to_left.start()

    def partner(k):
        if tiles & (tiles - 1):
            return lax.rem(t + k, tiles)
        bit, peer = 1, 0
        while bit < tiles:
            peer = peer + lax.rem(t // bit + k // bit, 2) * bit
            bit *= 2
        return peer

    def tpl_copy(k):
        return pltpu.make_async_remote_copy(
            src_ref=tpl.at[0, 0], dst_ref=stack.at[k], send_sem=tpl_send.at[k],
            recv_sem=tpl_recv.at[k], device_id={"tile": partner(k)},
            device_id_type=MESH,
        )

    def w_copy(k):
        return pltpu.make_async_remote_copy(
            src_ref=wbuf.at[0], dst_ref=wbuf.at[k], send_sem=w_send.at[k],
            recv_sem=w_recv.at[k], device_id={"tile": partner(k)},
            device_id_type=MESH,
        )

    tpl_copy(1).start()
    for k in range(1, tiles):
        w_copy(k).start()

    mask_rows, mask_cols = mask.shape
    row_id = lax.broadcasted_iota(jnp.int32, (share, mask_rows), 0) + o * share
    pick = lax.broadcasted_iota(jnp.int32, (share, mask_rows), 1)
    low_edge = pick * MBLK
    rows_of = jnp.where((row_id >= low_edge) & (row_id < low_edge + MBLK), 1.0, 0.0).astype(F32)
    col_id = lax.broadcasted_iota(jnp.int32, (mask_cols, side), 1)
    col_edge = lax.broadcasted_iota(jnp.int32, (mask_cols, side), 0) * MBLK
    cols_of = jnp.where((col_id >= col_edge) & (col_id < col_edge + MBLK), 1.0, 0.0).astype(F32)
    unmasked = 1.0 - dot(dot(rows_of, mask[...].astype(F32)), cols_of)

    tpl_copy(1).wait()
    spectrum(1)

    @pl.when(t < tiles - 1)
    def _():
        to_right.wait_send()
        to_left.wait_recv()

    @pl.when(t == tiles - 1)
    def _():
        halo_r[...] = jnp.zeros(halo_r.shape, F32)

    @pl.when(t > 0)
    def _():
        to_left.wait_send()
        to_right.wait_recv()

    @pl.when(t == 0)
    def _():
        halo_l[...] = jnp.zeros(halo_l.shape, F32)

    for k in range(2, tiles):
        tpl_copy(k).start()

    left, right = halo_l[...], halo_r[...]
    rolled = [pltpu.roll(mic[:, b * patch:(b + 1) * patch], guard, 1) for b in range(blocks)]
    rolled = (
        [jnp.concatenate([left, pltpu.roll(left, guard, 1)], axis=0)]
        + rolled
        + [jnp.concatenate([pltpu.roll(right, guard, 1), right], axis=0)]
    )
    lane = lax.broadcasted_iota(jnp.int32, (extent, patch), 1)
    ext = [jnp.where(lane < guard, rolled[b], rolled[b + 1]) for b in range(blocks + 1)]
    real, imag = [], []
    for b in range(blocks):
        half = right_table(jnp.concatenate([ext[b], ext[b + 1]], axis=1), tx)
        real.append(half[:, :patch])
        imag.append(half[:, patch:])
    real_high, real_low = split(jnp.concatenate(real, axis=1))
    imag_high, imag_low = split(jnp.concatenate(imag, axis=1))
    loads["ty"].wait()
    for a in range(blocks):
        rows = slice(a * patch, a * patch + length)
        img[a] = left_table(
            ty,
            jnp.concatenate([real_high[rows], imag_high[rows]], axis=0),
            jnp.concatenate([real_low[rows], imag_low[rows]], axis=0),
        )

    loads["ix"].wait()
    loads["iy"].wait()

    def correlate(k, a):
        sr, si = spec[k, :length], spec[k, length:]
        wide_r = jnp.concatenate([sr] * blocks, axis=1)
        wide_i = jnp.concatenate([si] * blocks, axis=1)
        weight = wbuf[k][:1, :1]
        ir, ii = img[a, :length, :], img[a, length:, :]
        cross = jnp.concatenate([ir * wide_r + ii * wide_i, ii * wide_r - ir * wide_i], axis=0)
        high, low = split(cross)
        mid = left_table(iy, high, low)
        pieces = jnp.concatenate(
            [
                jnp.concatenate(
                    [mid[:patch, b * patch:(b + 1) * patch], mid[patch:, b * patch:(b + 1) * patch]],
                    axis=1,
                )
                for b in range(blocks)
            ],
            axis=0,
        )
        final = right_table(pieces, ix) + weight
        for b in range(blocks):
            scores[k, :, b * patch:(b + 1) * patch] = final[b * patch:(b + 1) * patch]

    def own_lse(place):
        rows = pl.ds(pl.multiple_of(place * share, share), share)
        top = scores[0, rows, :]
        for k in range(1, tiles):
            top = jnp.maximum(top, scores[k, rows, :])
        total = jnp.exp(scores[0, rows, :] - top)
        for k in range(1, tiles):
            total = total + jnp.exp(scores[k, rows, :] - top)
        return top + jnp.log(total)

    def lse_copy(k):
        return pltpu.make_async_remote_copy(
            src_ref=lse_out.at[k], dst_ref=lse_in.at[k], send_sem=lse_send.at[k],
            recv_sem=lse_recv.at[k], device_id={"orient": lax.rem(o + k, orients)},
            device_id_type=MESH,
        )

    owners = patch // share
    home, seat = o // owners, lax.rem(o, owners)

    def send_rows(a, place):
        ahead = lax.rem(a * owners + place - o + orients, orients)
        lse_out[ahead] = own_lse(place)
        lse_copy(ahead).start()

    for s in range(blocks):
        a = lax.rem(home + 1 + s, blocks)
        if tiles <= 4:
            for k in range(tiles):
                if s == 0 and k:
                    w_copy(k).wait()
                if s == 0 and k > 1:
                    tpl_copy(k).wait()
                    spectrum(k)
                correlate(k, a)
        else:
            if s == 0:
                w_copy(1).wait()
                for k in range(2, tiles):
                    tpl_copy(k).wait()
                    w_copy(k).wait()

                def later(k, carry):
                    spectrum(k)
                    return carry

                lax.fori_loop(2, tiles, later, 0)

            def step(k, carry):
                correlate(k, a)
                return carry

            lax.fori_loop(0, tiles, step, 0)
        if s < blocks - 1:
            for place in range(owners):
                send_rows(a, place)
        else:
            for gap in range(1, owners):
                send_rows(a, lax.rem(seat + gap, owners))
    mine = own_lse(seat)
    for k in range(1, orients):
        lse_copy(k).wait()
    top = mine
    for k in range(1, orients):
        top = jnp.maximum(top, lse_in[k])
    total = jnp.exp(mine - top)
    for k in range(1, orients):
        total = total + jnp.exp(lse_in[k] - top)
    lse = top + jnp.log(total)

    def whole_sum(value):
        return jnp.sum(jnp.sum(value, axis=0, keepdims=True), axis=1, keepdims=True)

    count = whole_sum(unmasked)
    sum_here = whole_sum(unmasked * lse)
    mean_here = sum_here / jnp.maximum(count, 1.0)
    deviation = lse - mean_here
    squares = whole_sum(unmasked * deviation * deviation)
    lane = lax.broadcasted_iota(jnp.int32, stats.shape[1:], 1)
    stats[0] = jnp.where(
        lane == 0, count, jnp.where(lane == 1, sum_here, jnp.where(lane == 2, squares, 0.0))
    )

    def st_copy(k):
        peer = lax.rem(me + k, everyone)
        return pltpu.make_async_remote_copy(
            src_ref=stats.at[0], dst_ref=stats.at[k], send_sem=st_send.at[k],
            recv_sem=st_recv.at[k],
            device_id={"tile": peer // orients, "orient": lax.rem(peer, orients)},
            device_id_type=MESH,
        )

    def st_start(k, carry):
        st_copy(k).start()
        return carry

    def st_wait(k, carry):
        st_copy(k).wait()
        return carry

    lax.fori_loop(1, everyone, st_start, 0)
    lax.fori_loop(1, everyone, st_wait, 0)
    table = stats[:, 0, :]
    counts, sums, sqs = table[:, 0:1], table[:, 1:2], table[:, 2:3]
    live = jnp.sum(counts, axis=0, keepdims=True)
    average = jnp.sum(sums, axis=0, keepdims=True) / live
    gap = sums / jnp.maximum(counts, 1.0) - average
    variance = jnp.sum(sqs + counts * gap * gap, axis=0, keepdims=True) / live
    out[...] = unmasked * (lse - average) / jnp.sqrt(variance + 1e-05)


def body(tiles, orients, micrograph, templates, orient_ids, log_weight, ice_mask):
    extent, side = micrograph.shape
    patch = templates.shape[2]
    share = side // orients
    blocks = side // patch
    everyone = tiles * orients
    vmem = pl.BlockSpec(memory_space=pltpu.VMEM)
    dma = pltpu.SemaphoreType.DMA
    consts = [jnp.asarray(table) for table in tables(patch)]
    return pl.pallas_call(
        functools.partial(kernel, tiles, orients, patch // 2),
        out_shape=jax.ShapeDtypeStruct((share, side), F32),
        in_specs=[vmem] * 5 + [pl.BlockSpec(memory_space=pl.ANY)] * len(consts),
        out_specs=vmem,
        scratch_shapes=[
            *[pltpu.VMEM(table.shape, BF16) for table in consts],
            pltpu.VMEM((extent // 2, patch), F32),
            pltpu.VMEM((extent // 2, patch), F32),
            pltpu.VMEM((extent // 2, patch), F32),
            pltpu.VMEM((extent // 2, patch), F32),
            pltpu.VMEM((tiles, patch, patch), F32),
            pltpu.VMEM((tiles, 8, 128), F32),
            pltpu.VMEM((blocks, 4 * patch, side), F32),
            pltpu.VMEM((tiles, 4 * patch, patch), F32),
            pltpu.VMEM((tiles, patch, side), F32),
            pltpu.VMEM((orients, share, side), F32),
            pltpu.VMEM((orients, share, side), F32),
            pltpu.VMEM((everyone, 1, 128), F32),
            dma((len(consts),)),
            dma((2,)), dma((2,)),
            dma((tiles,)), dma((tiles,)), dma((tiles,)), dma((tiles,)),
            dma((orients,)), dma((orients,)),
            dma((everyone,)), dma((everyone,)),
        ],
        compiler_params=pltpu.CompilerParams(
            collective_id=0, has_side_effects=True, vmem_limit_bytes=56 * 1024 * 1024
        ),
    )(micrograph, templates, orient_ids, log_weight.reshape(1, -1), ice_mask, *consts)


def solution(mesh):
    return jax.shard_map(
        functools.partial(body, mesh.shape["tile"], mesh.shape["orient"]),
        mesh=mesh,
        in_specs=(
            P("group", "tile"),
            P("orient", "tile", None, None),
            P("orient", "tile"),
            P(),
            P("group", "tile"),
        ),
        out_specs=P(("group", "orient"), "tile"),
        check_vma=False,
    )
```
